256 devices in a mesh: span: 64 (over x, z, core), head: 4 (over y).
Axes of the slice: x: 4, y: 4, z: 8, core: 2. Of those that a mesh axis runs over, the one named last changes fastest.
Arguments:
- query: bfloat16 [131072, 2048], P('span', 'head'), may hold values from -27 to 27
- keys: bfloat16 [128, 128, 2048], P('span', 'head'), may hold values from -11 to 11
- values: bfloat16 [128, 128, 2048], P('span', 'head'), may hold values from -6 to 6
- grad_out: bfloat16 [131072, 2048], P('span', 'head'), may hold values from -6 to 6
- neighbour: int32 [2048], replicated, may hold values from 0 to 127, as said below
Outputs:
- attended: bfloat16 [131072, 2048], P('span', 'head')
- grad_query: bfloat16 [131072, 2048], P('span', 'head')
- grad_keys: bfloat16 [128, 128, 2048], P('span', 'head')
- grad_values: bfloat16 [128, 128, 2048], P('span', 'head')
The draws below stay inside these ranges and needn't reach their ends.
Inputs may be any that keep to these rules, and one draw needn't show every extreme that they name: Neighbour m is owned by index m // 2 of span, the block of keys and values that holds it. Among the 32 spans of one index of span at most one names a neighbour of any given owner, and some owner is named by exactly one span of every index of span.
All inputs are finite; a program needn't handle non-finite values.
Results may differ from the reference program's by a relative error of at most 0.03.
Values may be sent and summed in bfloat16 or wider, within the bound.
No kernel may reach another device: no remote copies, remote signals or barrier semaphores. Data moves between devices by JAX's collectives and lax.ppermute only.
A program may use at most 128 MiB of HBM per device.

```python
import math
import jax
import jax.numpy as jnp
from jax import lax

HEADS = 16
HS = 128
SPAN = 64
NBLEN = 128
CH_DEV = 32
NB_DEV = 2
OWNERS = 64
CAP = 1
NEIGH = 128
TOKENS = 131072
N_SPAN = 64


def neighbour_ids(key):
    base_key = jax.random.fold_in(key, 11)
    hot_key, block_key = jax.random.split(base_key, 2)
    hot_owner = jax.random.randint(hot_key, (), 0, OWNERS)
    item_owner = jnp.arange(OWNERS * CAP, dtype=jnp.int32) % OWNERS

    def one_block(inner_key):
        order_key, shuffle_key, local_key = jax.random.split(inner_key, 3)
        item_order = jax.random.permutation(order_key, OWNERS * CAP).astype(jnp.int32)
        item_score = jnp.where(item_owner == hot_owner, item_order - OWNERS * CAP, item_order)
        picked = jnp.argsort(item_score, stable=True)[:CH_DEV]
        chosen = item_owner[picked]
        shuffled = chosen[jax.random.permutation(shuffle_key, CH_DEV)]
        local_index = jax.random.randint(local_key, (CH_DEV,), 0, NB_DEV)
        return (shuffled * NB_DEV + local_index).astype(jnp.int32)
    blocks = jax.vmap(one_block)(jax.random.split(block_key, OWNERS))
    return blocks.reshape(-1).astype(jnp.int32)


def key_tensor(key):
    base_key = jax.random.fold_in(key, 23)
    first_key = jax.random.fold_in(base_key, 0)
    shape_all = (NEIGH, NBLEN, HEADS * HS)
    return jnp.clip(jax.random.normal(first_key, shape_all, jnp.float32), -4.0, 4.0)


def draw_neighbour(key, part):
    return neighbour_ids(key)


def draw_keys(key, part):
    return key_tensor(key).astype(jnp.bfloat16)


def draw_query(key, part):
    base_key = jax.random.fold_in(key, 37)
    first_key = jax.random.fold_in(base_key, 0)
    shape_all = (TOKENS, HEADS * HS)
    return jnp.clip(jax.random.normal(first_key, shape_all, jnp.float32), -4.0, 4.0).astype(jnp.bfloat16)


def block_scale(own_key, dims, cuts, low, largest):
    factor_of = 1.0
    for position, parts in cuts:
        heights = jax.random.uniform(jax.random.fold_in(jax.random.fold_in(own_key, 6), position), (parts,), jnp.float32, low / len(cuts), largest / len(cuts))
        factor_of = factor_of * jnp.repeat(jnp.exp(heights), dims[position] // parts).reshape((-1,) + (1,) * (len(dims) - 1 - position))
    return factor_of


def normal_values(stream_key, shape, spread, limit, cuts=(), kind=jnp.bfloat16):
    values = spread * jax.random.normal(stream_key, shape, jnp.float32)
    if cuts:
        values = values * block_scale(stream_key, shape, cuts, -0.22, 0.18)
    return jnp.clip(values, -limit, limit).astype(kind)


def setup_inputs(seed: int = 0) -> dict:
    seeds = jax.random.split(jax.random.key(seed), 6)
    return {
        "query": draw_query(jax.random.fold_in(seeds[5], 71), 0),
        "keys": draw_keys(jax.random.fold_in(seeds[5], 71), 0),
        "values": normal_values(seeds[2], (NEIGH, NBLEN, HEADS * HS), 1.0, 6.0, ((0, 64), (1, 4))),
        "grad_out": normal_values(seeds[3], (TOKENS, HEADS * HS), 1.0, 6.0, ((0, 64), (1, 4))),
        "neighbour": draw_neighbour(jax.random.fold_in(seeds[5], 71), 0),
    }


def reference(query, keys, values, grad_out, neighbour):
    width_all = HEADS * HS
    inv_scale = 1.0 / math.sqrt(HS)
    query_blocks = query.reshape(N_SPAN, CH_DEV, SPAN, HEADS, HS)
    grad_blocks = grad_out.reshape(N_SPAN, CH_DEV, SPAN, HEADS, HS)
    id_blocks = neighbour.reshape(N_SPAN, CH_DEV).astype(jnp.int32)

    def block_step(carried, inputs):
        sum_keys, sum_values = carried
        query_block, grad_block, id_block = inputs
        key_block = jnp.take(keys, id_block, axis=0).reshape(CH_DEV, NBLEN, HEADS, HS).astype(jnp.float32)
        value_block = jnp.take(values, id_block, axis=0).reshape(CH_DEV, NBLEN, HEADS, HS).astype(jnp.float32)
        query_wide = query_block.astype(jnp.float32)
        grad_wide = grad_block.astype(jnp.float32)
        scores = jnp.einsum('cqhd,ckhd->chqk', query_wide, key_block) * inv_scale
        row_top = lax.optimization_barrier(jnp.max(scores, axis=-1, keepdims=True))
        expo = jnp.exp(scores - row_top)
        probs = expo / lax.optimization_barrier(jnp.sum(expo, axis=-1, keepdims=True))
        probs_low = probs.astype(jnp.bfloat16)
        attended = jnp.einsum('chqk,ckhd->cqhd', probs_low.astype(jnp.float32), value_block).astype(jnp.bfloat16)
        delta_row = jnp.transpose(lax.optimization_barrier(jnp.sum(grad_wide * attended.astype(jnp.float32), axis=-1)), (0, 2, 1))
        dprobs = jnp.einsum('cqhd,ckhd->chqk', grad_wide, value_block)
        dscores = (probs * (dprobs - delta_row[..., None])).astype(jnp.bfloat16)
        dscores_wide = dscores.astype(jnp.float32)
        grad_query = (jnp.einsum('chqk,ckhd->cqhd', dscores_wide, key_block) * inv_scale).astype(jnp.bfloat16)
        key_terms = jnp.einsum('chqk,cqhd->ckhd', dscores_wide, query_wide)
        value_terms = jnp.einsum('chqk,cqhd->ckhd', probs_low.astype(jnp.float32), grad_wide)
        sum_keys = sum_keys.at[id_block].add(key_terms.reshape(CH_DEV, NBLEN, width_all))
        sum_values = sum_values.at[id_block].add(value_terms.reshape(CH_DEV, NBLEN, width_all))
        return ((sum_keys, sum_values), (attended, grad_query))
    zeros_start = jnp.zeros((NEIGH, NBLEN, width_all), jnp.float32)
    (sum_keys, sum_values), (attended, grad_query) = lax.scan(block_step, (zeros_start, zeros_start), (query_blocks, grad_blocks, id_blocks))
    return (attended.reshape(TOKENS, width_all), grad_query.reshape(TOKENS, width_all), (sum_keys * inv_scale).astype(jnp.bfloat16), sum_values.astype(jnp.bfloat16))
```

```python
import math

import jax
import jax.numpy as jnp
from jax import lax
from jax.experimental import pallas as pl
from jax.experimental.pallas import tpu as pltpu
from jax.sharding import Mesh, PartitionSpec as P

HS = 128
SPAN = 64
NBLEN = 128
X, Z, C = 4, 8, 2
NB = 2
SLOTS = X * Z * C * NB
GROUP = X * NB
STEP_SPANS = 8
SCALE = 1.0 / math.sqrt(HS)
SCALE_LOG2 = SCALE * math.log2(math.e)
BF = jnp.bfloat16
F32 = jnp.float32


def shift(a, axis, size, by):
    return lax.ppermute(a, axis, [(i, (i + by) % size) for i in range(size)])


def ring_gather(block):
    half = GROUP // 2
    parts = [block]
    right = left = block
    for _ in range(Z // 2 - 1):
        right = shift(right, "z", Z, 1)
        left = shift(left, "z", Z, -1)
        parts += [right, left]
    parts += [shift(right[:half], "z", Z, 1), shift(left[half:], "z", Z, -1)]
    return parts


def part_places():
    places = [(0, 0, GROUP)]
    for s in range(1, Z // 2):
        places += [(Z - s, 0, GROUP), (s, 0, GROUP)]
    half = GROUP // 2
    return places + [(Z // 2, 0, half), (Z // 2, half, half)]


PLACES = part_places()
N_PARTS = len(PLACES)


def ring_reduce(blocks):
    half = GROUP // 2
    far = blocks[Z // 2]
    right = shift(far[:half], "z", Z, 1)
    left = shift(far[half:], "z", Z, -1)
    right = jnp.concatenate([right + blocks[3][:half], blocks[3][half:]])
    left = jnp.concatenate([blocks[Z - 3][:half], left + blocks[Z - 3][half:]])
    for k in (2, 1):
        right = shift(right, "z", Z, 1) + blocks[k]
        left = shift(left, "z", Z, -1) + blocks[Z - k]
    right = shift(right, "z", Z, 1)
    left = shift(left, "z", Z, -1)
    return (right.astype(F32) + left.astype(F32) + blocks[0].astype(F32)).astype(BF)


def attention_kernel(ids_ref, q_ref, g_ref, *refs):
    k_parts, v_parts = refs[: 2 * N_PARTS], refs[2 * N_PARTS : 4 * N_PARTS]
    att_ref, gq_ref, dk_out, dv_out = refs[4 * N_PARTS : 4 * N_PARTS + 4]
    kbuf, vbuf, dk, dv, sems = refs[4 * N_PARTS + 4 :]
    step = pl.program_id(0)

    @pl.when(step == 0)
    def _():
        copies = []
        for which, (parts, buf) in enumerate(((k_parts, kbuf), (v_parts, vbuf))):
            for i, part in enumerate(parts):
                core, place = divmod(i, N_PARTS)
                offset, first, rows = PLACES[place]
                at = core * (Z * GROUP) + offset * GROUP + first
                copies.append(
                    pltpu.make_async_copy(
                        part, buf.at[pl.ds(at, rows)], sems.at[which * 2 * N_PARTS + i]
                    )
                )
        for copy in copies:
            copy.start()

        def clear(i, _):
            dk[i] = jnp.zeros((NBLEN, HS), F32)
            dv[i] = jnp.zeros((NBLEN, HS), F32)
            return 0

        lax.fori_loop(0, SLOTS, clear, 0)
        for copy in copies:
            copy.wait()

    def dot(a, b, ca, cb):
        return lax.dot_general(a, b, (((ca,), (cb,)), ((), ())), preferred_element_type=F32)

    def spans(first, count):
        rows = [pl.ds((first + i) * SPAN, SPAN) for i in range(count)]
        ids = [ids_ref[step * STEP_SPANS + first + i] for i in range(count)]
        qs = [q_ref[r, :] for r in rows]
        gs = [g_ref[r, :] for r in rows]
        scores = [dot(q, kbuf[n], 1, 1) * SCALE_LOG2 for q, n in zip(qs, ids)]
        dprobs = [dot(g, vbuf[n], 1, 1) for g, n in zip(gs, ids)]
        expo = [jnp.exp2(s - jnp.max(s, axis=-1, keepdims=True)) for s in scores]
        probs = [e * (1.0 / jnp.sum(e, axis=-1, keepdims=True)) for e in expo]
        low = [p.astype(BF) for p in probs]
        att = [dot(p, vbuf[n], 1, 0).astype(BF) for p, n in zip(low, ids)]
        for r, a in zip(rows, att):
            att_ref[r, :] = a
        delta = [
            jnp.sum(g.astype(F32) * a.astype(F32), axis=-1, keepdims=True) for g, a in zip(gs, att)
        ]
        ds = [(p * (d - t)).astype(BF) for p, d, t in zip(probs, dprobs, delta)]
        for r, d, n in zip(rows, ds, ids):
            gq_ref[r, :] = (dot(d, kbuf[n], 1, 0) * SCALE).astype(BF)
        value_terms = [dot(p, g, 0, 0) for p, g in zip(low, gs)]
        key_terms = [dot(d, q, 0, 0) for d, q in zip(ds, qs)]
        for n, vt, kt in zip(ids, value_terms, key_terms):
            dv[n] += vt
            dk[n] += kt

    for first in range(0, STEP_SPANS, 4):
        spans(first, 4)

    @pl.when(step == pl.num_programs(0) - 1)
    def _():
        def finish(i, _):
            dk_out[i] = (dk[i] * SCALE).astype(BF)
            dv_out[i] = dv[i].astype(BF)
            return 0

        lax.fori_loop(0, SLOTS, finish, 0)


def attention(ids, q, g, k_parts, v_parts):
    tokens = q.shape[0]
    rows = STEP_SPANS * SPAN
    token_spec = pl.BlockSpec((rows, HS), lambda i, ids: (i, 0))
    whole = pl.BlockSpec((SLOTS, NBLEN, HS), lambda i, ids: (0, 0, 0), pipeline_mode=pl.Buffered(1))
    any_spec = pl.BlockSpec(memory_space=pl.ANY)
    parts = list(k_parts) + list(v_parts)
    token_shape = jax.ShapeDtypeStruct((tokens, HS), BF)
    sum_shape = jax.ShapeDtypeStruct((SLOTS, NBLEN, HS), BF)
    return pl.pallas_call(
        attention_kernel,
        grid_spec=pltpu.PrefetchScalarGridSpec(
            num_scalar_prefetch=1,
            grid=(tokens // rows,),
            in_specs=[token_spec, token_spec] + [any_spec] * len(parts),
            out_specs=[token_spec, token_spec, whole, whole],
            scratch_shapes=[
                pltpu.VMEM((SLOTS, NBLEN, HS), BF),
                pltpu.VMEM((SLOTS, NBLEN, HS), BF),
                pltpu.VMEM((SLOTS, NBLEN, HS), F32),
                pltpu.VMEM((SLOTS, NBLEN, HS), F32),
                pltpu.SemaphoreType.DMA((len(parts),)),
            ],
        ),
        out_shape=[token_shape, token_shape, sum_shape, sum_shape],
        compiler_params=pltpu.CompilerParams(vmem_limit_bytes=56 * 1024 * 1024),
        name="attention",
    )(ids, q, g, *parts)


def per_device(query, keys, values, grad_out, neighbour):
    z_self, c_self = lax.axis_index("z"), lax.axis_index("core")
    tokens_here = query.shape[0]

    def encodings_out(a):
        return jnp.transpose(a.reshape(NB, NBLEN // 4, 16, HS), (2, 0, 1, 3))

    both = jnp.stack([encodings_out(keys), encodings_out(values)], axis=1)
    both = lax.all_to_all(both, ("head", "x"), split_axis=0, concat_axis=0, tiled=True)
    both = both.reshape(4, X, 2, NB, NBLEN // 4, HS)
    both = jnp.transpose(both, (2, 1, 3, 0, 4, 5)).reshape(2, GROUP, NBLEN, HS)

    def tokens_out(a):
        by_head = jnp.transpose(a.reshape(tokens_here, X, HS), (1, 0, 2))
        return lax.all_to_all(by_head, "x", split_axis=0, concat_axis=0, tiled=True).reshape(
            X * tokens_here, HS
        )

    q = tokens_out(query)
    g = tokens_out(grad_out)

    k_parts = ring_gather(both[0])
    v_parts = ring_gather(both[1])
    k_parts = k_parts + [shift(p, "core", C, 1) for p in k_parts]
    v_parts = v_parts + [shift(p, "core", C, 1) for p in v_parts]

    table = neighbour.reshape(X, Z, C, -1)
    table = lax.dynamic_index_in_dim(table, z_self, 1, keepdims=False)
    table = lax.dynamic_index_in_dim(table, c_self, 1, keepdims=False).reshape(-1)
    owner, local = table // NB, table % NB
    owner_x, owner_z, owner_c = owner // (Z * C), (owner // C) % Z, owner % C
    other = (owner_c != c_self).astype(jnp.int32)
    ids = ((other * Z + (owner_z - z_self) % Z) * X + owner_x) * NB + local

    att, gq, dk, dv = attention(ids, q, g, k_parts, v_parts)

    def tokens_back(a):
        back = lax.all_to_all(
            a.reshape(X, tokens_here, HS), "x", split_axis=0, concat_axis=0, tiled=True
        )
        return jnp.transpose(back, (1, 0, 2)).reshape(tokens_here, X * HS)

    def reduced(sums):
        sums = sums.reshape(C, Z, GROUP, NBLEN, HS)
        got = shift(sums[1], "core", C, 1)
        return ring_reduce([sums[0, k] + got[k] for k in range(Z)])

    grads = jnp.stack([reduced(dk), reduced(dv)])
    grads = grads.reshape(2, X, NB, 4, NBLEN // 4, HS)
    grads = jnp.transpose(grads, (3, 1, 0, 2, 4, 5)).reshape(16, 2, NB, NBLEN // 4, HS)
    grads = lax.all_to_all(grads, ("head", "x"), split_axis=0, concat_axis=0, tiled=True)
    grads = jnp.transpose(grads, (1, 2, 3, 0, 4)).reshape(2, NB, NBLEN // 4, 16 * HS)
    return tokens_back(att), tokens_back(gq), grads[0], grads[1]


def solution(mesh):
    fine = Mesh(mesh.devices.reshape(X, Z, C, 4), ("x", "z", "core", "head"))
    span = ("x", "z", "core")
    tokens, encodings = P(span, "head"), P(span, "head", None)
    return jax.shard_map(
        per_device,
        mesh=fine,
        in_specs=(tokens, encodings, encodings, tokens, P()),
        out_specs=(tokens, tokens, encodings, encodings),
        check_vma=False,
    )
```

```python
import math

import jax
import jax.numpy as jnp
from jax import lax
from jax.experimental import pallas as pl
from jax.experimental.pallas import tpu as pltpu
from jax.sharding import Mesh, PartitionSpec as P

HS = 128
SPAN = 64
NBLEN = 128
X, Y, Z, C = 4, 4, 8, 2
NB = 2
GROUP = X * NB
HALF = Z * GROUP
SLOTS = C * HALF
HEADS = X * Y
PIECE = NBLEN // Y
SCALE = 1.0 / math.sqrt(HS)
SCALE_LOG2 = SCALE * math.log2(math.e)
BF = jnp.bfloat16
F32 = jnp.float32
EARLY, LATE = (0, 7, 1, 6, 2), (5, 3, 4)
ORDER = EARLY + LATE
N_EARLY, N_LATE = len(EARLY) * GROUP, len(LATE) * GROUP
BATCH = 16
MIB = 1024 * 1024


def shift(a, axis, size, by):
    return lax.ppermute(a, axis, [(i, (i + by) % size) for i in range(size)])


def ring_gather(block):
    half = GROUP // 2
    right1, left1 = shift(block, "z", Z, 1), shift(block, "z", Z, -1)
    right2, left2 = shift(right1, "z", Z, 1), shift(left1, "z", Z, -1)
    early = jnp.concatenate([block, right1, left1, right2, left2])
    right3, left3 = shift(right2, "z", Z, 1), shift(left2, "z", Z, -1)
    far = [shift(right3[:half], "z", Z, 1), shift(left3[half:], "z", Z, -1)]
    late = jnp.concatenate([right3, left3] + far)
    return early, late


def ring_reduce(blocks):
    half = GROUP // 2
    far = blocks[Z // 2]
    right = shift(far[:half], "z", Z, 1)
    left = shift(far[half:], "z", Z, -1)
    right = jnp.concatenate([right + blocks[3][:half], blocks[3][half:]])
    left = jnp.concatenate([blocks[Z - 3][:half], left + blocks[Z - 3][half:]])
    for k in (2, 1):
        right = shift(right, "z", Z, 1) + blocks[k]
        left = shift(left, "z", Z, -1) + blocks[Z - k]
    return shift(right, "z", Z, 1), shift(left, "z", Z, -1)


def dot(a, b, ca, cb):
    return lax.dot_general(a, b, (((ca,), (cb,)), ((), ())), preferred_element_type=F32)


def attention_kernel(ids, tokens, *refs):
    keys, values = refs[:4], refs[4:8]
    reply, dk_outs, dv_outs = refs[8], refs[9:12], refs[12:15]
    tbuf, kbuf, vbuf, obuf, dk, dv, low, t_sems, kv_sems, o_sems, s_sems = refs[15:]
    loads = []
    for sources, buf in ((keys, kbuf), (values, vbuf)):
        at = 0
        for source in sources:
            rows = source.shape[0]
            loads.append(
                pltpu.make_async_copy(source, buf.at[pl.ds(at, rows)], kv_sems.at[len(loads)])
            )
            at += rows

    def token_load(part):
        return pltpu.make_async_copy(tokens.at[part], tbuf.at[part], t_sems.at[part])

    def token_store(part):
        return pltpu.make_async_copy(obuf.at[part], reply.at[part], o_sems.at[part])

    for load in loads:
        load.start()
    for part in range(X):
        token_load(part).start()

    def clear(i, _):
        dk[i] = jnp.zeros((NBLEN, HS), F32)
        dv[i] = jnp.zeros((NBLEN, HS), F32)
        return 0

    lax.fori_loop(0, SLOTS, clear, 0, unroll=2)
    for load in loads:
        load.wait()
    steps_per_part = tokens.shape[2] // (BATCH * SPAN)

    def body(step, _):
        part, inner = step // steps_per_part, step % steps_per_part

        @pl.when(inner == 0)
        def _():
            token_load(part).wait()

        q_ref, g_ref = tbuf.at[part, 0], tbuf.at[part, 1]
        att_ref, gq_ref = obuf.at[part, 0], obuf.at[part, 1]
        rows = [
            pl.ds(pl.multiple_of((inner * BATCH + i) * SPAN, SPAN), SPAN) for i in range(BATCH)
        ]
        named = [ids[step * BATCH + i] for i in range(BATCH)]
        qs = [q_ref[r, :] for r in rows]
        gs = [g_ref[r, :] for r in rows]
        scores = [dot(q, kbuf[n], 1, 1) * SCALE_LOG2 for q, n in zip(qs, named)]
        dprobs = [dot(g, vbuf[n], 1, 1) for g, n in zip(gs, named)]
        expo = [jnp.exp2(s - jnp.max(s, axis=-1, keepdims=True)) for s in scores]
        probs = [e * (1.0 / jnp.sum(e, axis=-1, keepdims=True)) for e in expo]
        probs_low = [p.astype(BF) for p in probs]
        att = [dot(p, vbuf[n], 1, 0).astype(BF) for p, n in zip(probs_low, named)]
        for r, a in zip(rows, att):
            att_ref[r, :] = a
        delta = [
            jnp.sum(g.astype(F32) * a.astype(F32), axis=-1, keepdims=True) for g, a in zip(gs, att)
        ]
        ds = [(p * (d - t)).astype(BF) for p, d, t in zip(probs, dprobs, delta)]
        for r, d, n in zip(rows, ds, named):
            gq_ref[r, :] = (dot(d, kbuf[n], 1, 0) * SCALE).astype(BF)
        value_terms = [dot(p, g, 0, 0) for p, g in zip(probs_low, gs)]
        key_terms = [dot(d, q, 0, 0) for d, q in zip(ds, qs)]
        for n, vt, kt in zip(named, value_terms, key_terms):
            dv[n] += vt
            dk[n] += kt

        @pl.when(inner == steps_per_part - 1)
        def _():
            token_store(part).start()

        return 0

    lax.fori_loop(0, X * steps_per_part, body, 0)

    stores = []
    spans = ((HALF + N_EARLY, SLOTS), (HALF, HALF + N_EARLY), (0, HALF))
    for piece, (first, last) in enumerate(spans):
        for which, (sums, outs) in enumerate(((dk, dk_outs), (dv, dv_outs))):

            def finish(i, _):
                value = sums[i]
                low[which, i] = (value * SCALE if which == 0 else value).astype(BF)
                return 0

            lax.fori_loop(first, last, finish, 0, unroll=2)
            store = pltpu.make_async_copy(
                low.at[which, pl.ds(first, last - first)], outs[piece], s_sems.at[2 * piece + which]
            )
            store.start()
            stores.append(store)
    for store in stores:
        store.wait()
    for part in range(X):
        token_store(part).wait()


def attention(ids, tokens, parts):
    hbm = pl.BlockSpec(memory_space=pl.ANY)
    sums = [
        jax.ShapeDtypeStruct((n, NBLEN, HS), BF) for n in (N_LATE, N_EARLY, HALF)
    ]
    low = pltpu.VMEM((SLOTS, NBLEN, HS), BF)
    wide = pltpu.VMEM((SLOTS, NBLEN, HS), F32)
    dma = pltpu.SemaphoreType.DMA
    return pl.pallas_call(
        attention_kernel,
        grid_spec=pltpu.PrefetchScalarGridSpec(
            num_scalar_prefetch=1,
            grid=(1,),
            in_specs=[hbm] * 9,
            out_specs=[hbm] * 7,
            scratch_shapes=[
                pltpu.VMEM(tokens.shape, BF),
                low,
                low,
                pltpu.VMEM(tokens.shape, BF),
                wide,
                wide,
                pltpu.VMEM((2, SLOTS, NBLEN, HS), BF),
                dma((X,)),
                dma((8,)),
                dma((X,)),
                dma((6,)),
            ],
        ),
        out_shape=[jax.ShapeDtypeStruct(tokens.shape, BF)] + sums + sums,
        compiler_params=pltpu.CompilerParams(vmem_limit_bytes=56 * MIB),
        name="attention",
    )(ids, tokens, *parts)


def split_heads(a, b):
    tokens = a.shape[0]
    rows = 512

    def kernel(a_ref, b_ref, out):
        for h in range(X):
            at = pl.ds(h * HS, HS)
            out[h, 0] = a_ref[:, at]
            out[h, 1] = b_ref[:, at]

    wide = pl.BlockSpec((rows, X * HS), lambda i: (i, 0))
    return pl.pallas_call(
        kernel,
        grid=(tokens // rows,),
        in_specs=[wide, wide],
        out_specs=pl.BlockSpec((X, 2, rows, HS), lambda i: (0, 0, i, 0)),
        out_shape=jax.ShapeDtypeStruct((X, 2, tokens, HS), BF),
        name="split_heads",
    )(a, b)


def join_heads(a):
    tokens = a.shape[2]
    rows = 512

    def kernel(a_ref, out0, out1):
        for h in range(X):
            at = pl.ds(h * HS, HS)
            out0[:, at] = a_ref[h, 0]
            out1[:, at] = a_ref[h, 1]

    wide = pl.BlockSpec((rows, X * HS), lambda i: (i, 0))
    return pl.pallas_call(
        kernel,
        grid=(tokens // rows,),
        in_specs=[pl.BlockSpec((X, 2, rows, HS), lambda i: (0, 0, i, 0))],
        out_specs=[wide, wide],
        out_shape=[jax.ShapeDtypeStruct((tokens, X * HS), BF)] * 2,
        name="join_heads",
    )(a)


def pack_encodings(keys, values):
    def kernel(k_ref, v_ref, out):
        for h in range(HEADS):
            at = pl.ds(h * HS, HS)
            out[h, 0] = k_ref[:, :, at]
            out[h, 1] = v_ref[:, :, at]

    return pl.pallas_call(
        kernel,
        out_shape=jax.ShapeDtypeStruct((HEADS, 2, NB, PIECE, HS), BF),
        name="pack_encodings",
    )(keys, values)


def unpack_encodings(a):
    def kernel(a_ref, k_ref, v_ref):
        for h in range(HEADS):
            at = pl.ds(h * HS, HS)
            k_ref[:, :, at] = a_ref[h, 0]
            v_ref[:, :, at] = a_ref[h, 1]

    return pl.pallas_call(
        kernel,
        out_shape=[jax.ShapeDtypeStruct((NB, PIECE, HEADS * HS), BF)] * 2,
        name="unpack_encodings",
    )(a)


def final_sums(key_terms, value_terms):
    def kernel(*refs):
        out = refs[-1]
        for which in range(2):
            terms = refs[4 * which : 4 * which + 4]
            for x in range(X):
                for n in range(NB):
                    total = sum(t[x * NB + n].astype(F32) for t in terms).astype(BF)
                    for y in range(Y):
                        out[y, x, which, n] = total[y * PIECE : (y + 1) * PIECE]

    block = pl.BlockSpec((GROUP, NBLEN, HS), lambda i: (0, 0, 0))
    shape = (Y, X, 2, NB, PIECE, HS)
    return pl.pallas_call(
        kernel,
        grid=(1,),
        in_specs=[block] * 8,
        out_specs=pl.BlockSpec(shape, lambda i: (0,) * 6),
        out_shape=jax.ShapeDtypeStruct(shape, BF),
        name="final_sums",
    )(*key_terms, *value_terms)


def per_device(query, keys, values, grad_out, neighbour):
    z_self, c_self = lax.axis_index("z"), lax.axis_index("core")

    both = pack_encodings(keys, values)
    both = lax.all_to_all(both, ("head", "x"), split_axis=0, concat_axis=0, tiled=True)
    both = both.reshape(Y, X, 2, NB, PIECE, HS)
    both = jnp.transpose(both, (2, 1, 3, 0, 4, 5)).reshape(2, GROUP, NBLEN, HS)

    tokens = split_heads(query, grad_out)
    tokens = lax.all_to_all(tokens, "x", split_axis=0, concat_axis=0, tiled=True)

    parts = []
    for block in (both[0], both[1]):
        early, late = ring_gather(block)
        parts += [early, late, shift(early, "core", C, 1), shift(late, "core", C, 1)]

    table = neighbour.reshape(X, Z, C, -1)
    table = lax.dynamic_index_in_dim(table, z_self, 1, keepdims=False)
    table = lax.dynamic_index_in_dim(table, c_self, 1, keepdims=False).reshape(-1)
    owner, local = table // NB, table % NB
    owner_x, owner_z, owner_c = owner // (Z * C), (owner // C) % Z, owner % C
    other = (owner_c != c_self).astype(jnp.int32)
    offset = (owner_z - z_self) % Z
    place = sum(jnp.where(offset == o, i, 0) for i, o in enumerate(ORDER))
    ids = ((other * Z + place) * X + owner_x) * NB + local

    reply, *sums = attention(ids, tokens, parts)
    reply = lax.all_to_all(reply, "x", split_axis=0, concat_axis=0, tiled=True)

    terms = []
    for late, early, own in (sums[:3], sums[3:]):
        got_late, got_early = shift(late, "core", C, 1), shift(early, "core", C, 1)

        def block(k):
            place = ORDER.index(k)
            at = place * GROUP
            got = got_early[at : at + GROUP] if place < len(EARLY) else got_late[at - N_EARLY : at - N_EARLY + GROUP]
            return own[at : at + GROUP] + got

        right, left = ring_reduce([None] + [block(k) for k in range(1, Z)])
        terms.append((own, got_early, right, left))

    grads = final_sums(*terms).reshape(HEADS, 2, NB, PIECE, HS)
    grads, reply = lax.optimization_barrier((grads, reply))
    grads = lax.all_to_all(grads, ("head", "x"), split_axis=0, concat_axis=0, tiled=True)
    attended, grad_query = join_heads(reply)
    grad_keys, grad_values = unpack_encodings(grads)
    return attended, grad_query, grad_keys, grad_values


def solution(mesh):
    fine = Mesh(mesh.devices.reshape(X, Z, C, Y), ("x", "z", "core", "head"))
    span = ("x", "z", "core")
    tokens, encodings = P(span, "head"), P(span, "head", None)
    return jax.shard_map(
        per_device,
        mesh=fine,
        in_specs=(tokens, encodings, encodings, tokens, P()),
        out_specs=(tokens, tokens, encodings, encodings),
        check_vma=False,
    )
```

```python
import math

import jax
import jax.numpy as jnp
from jax import lax
from jax.experimental import pallas as pl
from jax.experimental.pallas import tpu as pltpu
from jax.sharding import Mesh, PartitionSpec as P

HS = 128
SPAN = 64
NBLEN = 128
X, Y, Z, C = 4, 4, 8, 2
NB = 2
GROUP = X * NB
HALF = Z * GROUP
SLOTS = C * HALF
HEADS = X * Y
PIECE = NBLEN // Y
SCALE = 1.0 / math.sqrt(HS)
SCALE_LOG2 = SCALE * math.log2(math.e)
BF = jnp.bfloat16
F32 = jnp.float32
EARLY, LATE = (0, 7, 1, 6, 2), (5, 3, 4)
ORDER = EARLY + LATE
N_EARLY, N_LATE = len(EARLY) * GROUP, len(LATE) * GROUP
BATCH = 32
MIB = 1024 * 1024


def shift(a, axis, size, by):
    return lax.ppermute(a, axis, [(i, (i + by) % size) for i in range(size)])


def ring_gather(block):
    half = GROUP // 2
    right1, left1 = shift(block, "z", Z, 1), shift(block, "z", Z, -1)
    right2, left2 = shift(right1, "z", Z, 1), shift(left1, "z", Z, -1)
    early = jnp.concatenate([block, right1, left1, right2, left2])
    right3, left3 = shift(right2, "z", Z, 1), shift(left2, "z", Z, -1)
    far = [shift(right3[:half], "z", Z, 1), shift(left3[half:], "z", Z, -1)]
    late = jnp.concatenate([right3, left3] + far)
    return early, late


def ring_reduce(blocks):
    half = GROUP // 2
    far = blocks[Z // 2]
    right = shift(far[:half], "z", Z, 1)
    left = shift(far[half:], "z", Z, -1)
    right = jnp.concatenate([right + blocks[3][:half], blocks[3][half:]])
    left = jnp.concatenate([blocks[Z - 3][:half], left + blocks[Z - 3][half:]])
    for k in (2, 1):
        right = shift(right, "z", Z, 1) + blocks[k]
        left = shift(left, "z", Z, -1) + blocks[Z - k]
    return shift(right, "z", Z, 1), shift(left, "z", Z, -1)


def dot(a, b, ca, cb):
    return lax.dot_general(a, b, (((ca,), (cb,)), ((), ())), preferred_element_type=F32)


def attention_kernel(ids, tokens, *refs):
    keys, values = refs[:4], refs[4:8]
    reply, dk_outs, dv_outs = refs[8], refs[9:12], refs[12:15]
    tbuf, kbuf, vbuf, obuf, dk, dv, low, t_sems, kv_sems, o_sems, s_sems = refs[15:]
    loads = []
    for sources, buf in ((keys, kbuf), (values, vbuf)):
        at = 0
        for source in sources:
            rows = source.shape[0]
            loads.append(
                pltpu.make_async_copy(source, buf.at[pl.ds(at, rows)], kv_sems.at[len(loads)])
            )
            at += rows

    def token_load(part):
        return pltpu.make_async_copy(tokens.at[part], tbuf.at[part], t_sems.at[part])

    def token_store(part):
        return pltpu.make_async_copy(obuf.at[part], reply.at[part], o_sems.at[part])

    for load in loads:
        load.start()
    for part in range(X):
        token_load(part).start()

    def clear(i, _):
        dk[i] = jnp.zeros((NBLEN, HS), F32)
        dv[i] = jnp.zeros((NBLEN, HS), F32)
        return 0

    lax.fori_loop(0, SLOTS, clear, 0, unroll=2)
    for load in loads:
        load.wait()
    steps_per_part = tokens.shape[2] // (BATCH * SPAN)

    def body(step, _):
        part, inner = step // steps_per_part, step % steps_per_part

        @pl.when(inner == 0)
        def _():
            token_load(part).wait()

        q_ref, g_ref = tbuf.at[part, 0], tbuf.at[part, 1]
        att_ref, gq_ref = obuf.at[part, 0], obuf.at[part, 1]
        rows = [
            pl.ds(pl.multiple_of((inner * BATCH + i) * SPAN, SPAN), SPAN) for i in range(BATCH)
        ]
        named = [ids[step * BATCH + i] for i in range(BATCH)]
        qs = [q_ref[r, :] for r in rows]
        gs = [g_ref[r, :] for r in rows]
        scores = [dot(q, kbuf[n], 1, 1) * SCALE_LOG2 for q, n in zip(qs, named)]
        dprobs = [dot(g, vbuf[n], 1, 1) for g, n in zip(gs, named)]
        expo = [jnp.exp2(s - jnp.max(s, axis=-1, keepdims=True)) for s in scores]
        probs = [e * (1.0 / jnp.sum(e, axis=-1, keepdims=True)) for e in expo]
        probs_low = [p.astype(BF) for p in probs]
        att = [dot(p, vbuf[n], 1, 0).astype(BF) for p, n in zip(probs_low, named)]
        for r, a in zip(rows, att):
            att_ref[r, :] = a
        delta = [
            jnp.sum(g.astype(F32) * a.astype(F32), axis=-1, keepdims=True) for g, a in zip(gs, att)
        ]
        ds = [(p * (d - t)).astype(BF) for p, d, t in zip(probs, dprobs, delta)]
        for r, d, n in zip(rows, ds, named):
            gq_ref[r, :] = (dot(d, kbuf[n], 1, 0) * SCALE).astype(BF)
        value_terms = [dot(p, g, 0, 0) for p, g in zip(probs_low, gs)]
        key_terms = [dot(d, q, 0, 0) for d, q in zip(ds, qs)]
        for n, vt, kt in zip(named, value_terms, key_terms):
            dv[n] += vt
            dk[n] += kt

        @pl.when(inner == steps_per_part - 1)
        def _():
            token_store(part).start()

        return 0

    lax.fori_loop(0, X * steps_per_part, body, 0)

    stores = []
    spans = ((HALF + N_EARLY, SLOTS), (HALF, HALF + N_EARLY), (0, HALF))
    for piece, (first, last) in enumerate(spans):
        for which, (sums, outs) in enumerate(((dk, dk_outs), (dv, dv_outs))):

            def finish(i, _):
                value = sums[i]
                low[which, i] = (value * SCALE if which == 0 else value).astype(BF)
                return 0

            lax.fori_loop(first, last, finish, 0, unroll=2)
            store = pltpu.make_async_copy(
                low.at[which, pl.ds(first, last - first)], outs[piece], s_sems.at[2 * piece + which]
            )
            store.start()
            stores.append(store)
    for store in stores:
        store.wait()
    for part in range(X):
        token_store(part).wait()


def attention(ids, tokens, parts):
    hbm = pl.BlockSpec(memory_space=pl.ANY)
    sums = [
        jax.ShapeDtypeStruct((n, NBLEN, HS), BF) for n in (N_LATE, N_EARLY, HALF)
    ]
    low = pltpu.VMEM((SLOTS, NBLEN, HS), BF)
    wide = pltpu.VMEM((SLOTS, NBLEN, HS), F32)
    dma = pltpu.SemaphoreType.DMA
    return pl.pallas_call(
        attention_kernel,
        grid_spec=pltpu.PrefetchScalarGridSpec(
            num_scalar_prefetch=1,
            grid=(1,),
            in_specs=[hbm] * 9,
            out_specs=[hbm] * 7,
            scratch_shapes=[
                pltpu.VMEM(tokens.shape, BF),
                low,
                low,
                pltpu.VMEM(tokens.shape, BF),
                wide,
                wide,
                pltpu.VMEM((2, SLOTS, NBLEN, HS), BF),
                dma((X,)),
                dma((8,)),
                dma((X,)),
                dma((6,)),
            ],
        ),
        out_shape=[jax.ShapeDtypeStruct(tokens.shape, BF)] + sums + sums,
        compiler_params=pltpu.CompilerParams(vmem_limit_bytes=56 * MIB),
        name="attention",
    )(ids, tokens, *parts)


def split_heads(a, b):
    tokens = a.shape[0]
    rows = 512

    def kernel(a_ref, b_ref, out):
        for h in range(X):
            at = pl.ds(h * HS, HS)
            out[h, 0] = a_ref[:, at]
            out[h, 1] = b_ref[:, at]

    wide = pl.BlockSpec((rows, X * HS), lambda i: (i, 0))
    return pl.pallas_call(
        kernel,
        grid=(tokens // rows,),
        in_specs=[wide, wide],
        out_specs=pl.BlockSpec((X, 2, rows, HS), lambda i: (0, 0, i, 0)),
        out_shape=jax.ShapeDtypeStruct((X, 2, tokens, HS), BF),
        name="split_heads",
    )(a, b)


def join_heads(a):
    tokens = a.shape[2]
    rows = 512

    def kernel(a_ref, out0, out1):
        for h in range(X):
            at = pl.ds(h * HS, HS)
            out0[:, at] = a_ref[h, 0]
            out1[:, at] = a_ref[h, 1]

    wide = pl.BlockSpec((rows, X * HS), lambda i: (i, 0))
    return pl.pallas_call(
        kernel,
        grid=(tokens // rows,),
        in_specs=[pl.BlockSpec((X, 2, rows, HS), lambda i: (0, 0, i, 0))],
        out_specs=[wide, wide],
        out_shape=[jax.ShapeDtypeStruct((tokens, X * HS), BF)] * 2,
        name="join_heads",
    )(a)


def pack_encodings(keys, values):
    def kernel(k_ref, v_ref, out):
        for h in range(HEADS):
            at = pl.ds(h * HS, HS)
            out[h, 0] = k_ref[:, :, at]
            out[h, 1] = v_ref[:, :, at]

    return pl.pallas_call(
        kernel,
        out_shape=jax.ShapeDtypeStruct((HEADS, 2, NB, PIECE, HS), BF),
        name="pack_encodings",
    )(keys, values)


def unpack_encodings(a):
    def kernel(a_ref, k_ref, v_ref):
        for h in range(HEADS):
            at = pl.ds(h * HS, HS)
            k_ref[:, :, at] = a_ref[h, 0]
            v_ref[:, :, at] = a_ref[h, 1]

    return pl.pallas_call(
        kernel,
        out_shape=[jax.ShapeDtypeStruct((NB, PIECE, HEADS * HS), BF)] * 2,
        name="unpack_encodings",
    )(a)


def final_sums(key_terms, value_terms):
    def kernel(*refs):
        out = refs[-1]
        for which in range(2):
            terms = refs[4 * which : 4 * which + 4]
            for x in range(X):
                for n in range(NB):
                    total = sum(t[x * NB + n].astype(F32) for t in terms).astype(BF)
                    for y in range(Y):
                        out[y, x, which, n] = total[y * PIECE : (y + 1) * PIECE]

    block = pl.BlockSpec((GROUP, NBLEN, HS), lambda i: (0, 0, 0))
    shape = (Y, X, 2, NB, PIECE, HS)
    return pl.pallas_call(
        kernel,
        grid=(1,),
        in_specs=[block] * 8,
        out_specs=pl.BlockSpec(shape, lambda i: (0,) * 6),
        out_shape=jax.ShapeDtypeStruct(shape, BF),
        name="final_sums",
    )(*key_terms, *value_terms)


def per_device(query, keys, values, grad_out, neighbour):
    z_self, c_self = lax.axis_index("z"), lax.axis_index("core")

    both = pack_encodings(keys, values)
    both = lax.all_to_all(both, ("head", "x"), split_axis=0, concat_axis=0, tiled=True)
    both = both.reshape(Y, X, 2, NB, PIECE, HS)
    both = jnp.transpose(both, (2, 1, 3, 0, 4, 5)).reshape(2, GROUP, NBLEN, HS)

    tokens = split_heads(query, grad_out)
    tokens = lax.all_to_all(tokens, "x", split_axis=0, concat_axis=0, tiled=True)

    parts = []
    for block in (both[0], both[1]):
        early, late = ring_gather(block)
        parts += [early, late, shift(early, "core", C, 1), shift(late, "core", C, 1)]

    table = neighbour.reshape(X, Z, C, -1)
    table = lax.dynamic_index_in_dim(table, z_self, 1, keepdims=False)
    table = lax.dynamic_index_in_dim(table, c_self, 1, keepdims=False).reshape(-1)
    owner, local = table // NB, table % NB
    owner_x, owner_z, owner_c = owner // (Z * C), (owner // C) % Z, owner % C
    other = (owner_c != c_self).astype(jnp.int32)
    offset = (owner_z - z_self) % Z
    place = sum(jnp.where(offset == o, i, 0) for i, o in enumerate(ORDER))
    ids = ((other * Z + place) * X + owner_x) * NB + local

    reply, *sums = attention(ids, tokens, parts)
    reply = lax.all_to_all(reply, "x", split_axis=0, concat_axis=0, tiled=True)

    terms = []
    for late, early, own in (sums[:3], sums[3:]):
        got_late, got_early = shift(late, "core", C, 1), shift(early, "core", C, 1)

        def block(k):
            place = ORDER.index(k)
            at = place * GROUP
            got = got_early[at : at + GROUP] if place < len(EARLY) else got_late[at - N_EARLY : at - N_EARLY + GROUP]
            return own[at : at + GROUP] + got

        right, left = ring_reduce([None] + [block(k) for k in range(1, Z)])
        terms.append((own, got_early, right, left))

    grads = final_sums(*terms).reshape(HEADS, 2, NB, PIECE, HS)
    grads, reply = lax.optimization_barrier((grads, reply))
    grads = lax.all_to_all(grads, ("head", "x"), split_axis=0, concat_axis=0, tiled=True)
    attended, grad_query = join_heads(reply)
    grad_keys, grad_values = unpack_encodings(grads)
    return attended, grad_query, grad_keys, grad_values


def solution(mesh):
    fine = Mesh(mesh.devices.reshape(X, Z, C, Y), ("x", "z", "core", "head"))
    span = ("x", "z", "core")
    tokens, encodings = P(span, "head"), P(span, "head", None)
    return jax.shard_map(
        per_device,
        mesh=fine,
        in_specs=(tokens, encodings, encodings, tokens, P()),
        out_specs=(tokens, tokens, encodings, encodings),
        check_vma=False,
    )
```

```python
import math

import jax
import jax.numpy as jnp
from jax import lax
from jax.experimental import pallas as pl
from jax.experimental.pallas import tpu as pltpu
from jax.sharding import Mesh, PartitionSpec as P

HS = 128
SPAN = 64
NBLEN = 128
X, Y, Z, C = 4, 4, 8, 2
NB = 2
GROUP = X * NB
HALF = Z * GROUP
SLOTS = C * HALF
HEADS = X * Y
PIECE = NBLEN // Y
SCALE = 1.0 / math.sqrt(HS)
SCALE_LOG2 = SCALE * math.log2(math.e)
BF = jnp.bfloat16
F32 = jnp.float32
EARLY, LATE = (0, 7, 1, 6, 2), (5, 3, 4)
ORDER = EARLY + LATE
N_EARLY, N_LATE = len(EARLY) * GROUP, len(LATE) * GROUP
BATCH = 32
MIB = 1024 * 1024


def shift(a, axis, size, by):
    return lax.ppermute(a, axis, [(i, (i + by) % size) for i in range(size)])


def ring_gather(block):
    half = GROUP // 2
    right1, left1 = shift(block, "z", Z, 1), shift(block, "z", Z, -1)
    right2, left2 = shift(right1, "z", Z, 1), shift(left1, "z", Z, -1)
    early = jnp.concatenate([block, right1, left1, right2, left2])
    right3, left3 = shift(right2, "z", Z, 1), shift(left2, "z", Z, -1)
    far = [shift(right3[:half], "z", Z, 1), shift(left3[half:], "z", Z, -1)]
    late = jnp.concatenate([right3, left3] + far)
    return early, late


def ring_reduce(blocks):
    half = GROUP // 2
    far = blocks[Z // 2]
    right = shift(far[:half], "z", Z, 1)
    left = shift(far[half:], "z", Z, -1)
    right = jnp.concatenate([right + blocks[3][:half], blocks[3][half:]])
    left = jnp.concatenate([blocks[Z - 3][:half], left + blocks[Z - 3][half:]])
    for k in (2, 1):
        right = shift(right, "z", Z, 1) + blocks[k]
        left = shift(left, "z", Z, -1) + blocks[Z - k]
    return shift(right, "z", Z, 1), shift(left, "z", Z, -1)


def dot(a, b, ca, cb):
    return lax.dot_general(a, b, (((ca,), (cb,)), ((), ())), preferred_element_type=F32)


def attention_kernel(ids, tokens, *refs):
    keys, values = refs[:4], refs[4:8]
    reply, dk_outs, dv_outs = refs[8], refs[9:12], refs[12:15]
    tbuf, kbuf, vbuf, obuf, dk, dv, low, t_sems, kv_sems, o_sems, s_sems = refs[15:]
    loads = []
    for sources, buf in ((keys, kbuf), (values, vbuf)):
        at = 0
        for source in sources:
            rows = source.shape[0]
            loads.append(
                pltpu.make_async_copy(source, buf.at[pl.ds(at, rows)], kv_sems.at[len(loads)])
            )
            at += rows

    def token_load(part):
        return pltpu.make_async_copy(tokens.at[part], tbuf.at[part], t_sems.at[part])

    def token_store(part):
        return pltpu.make_async_copy(obuf.at[part], reply.at[part], o_sems.at[part])

    for load in loads:
        load.start()
    token_load(0).start()

    def clear(i, _):
        dk[i] = jnp.zeros((NBLEN, HS), F32)
        dv[i] = jnp.zeros((NBLEN, HS), F32)
        return 0

    lax.fori_loop(0, SLOTS, clear, 0, unroll=2)
    for load in loads:
        load.wait()
    steps_per_part = tokens.shape[2] // (BATCH * SPAN)

    def body(step, _):
        part, inner = step // steps_per_part, step % steps_per_part

        @pl.when(inner == 0)
        def _():
            token_load(part).wait()

        @pl.when(jnp.logical_and(inner == 0, part + 1 < X))
        def _():
            token_load(part + 1).start()

        q_ref, g_ref = tbuf.at[part, 0], tbuf.at[part, 1]
        att_ref, gq_ref = obuf.at[part, 0], obuf.at[part, 1]
        rows = [
            pl.ds(pl.multiple_of((inner * BATCH + i) * SPAN, SPAN), SPAN) for i in range(BATCH)
        ]
        named = [ids[step * BATCH + i] for i in range(BATCH)]
        qs = [q_ref[r, :] for r in rows]
        gs = [g_ref[r, :] for r in rows]
        scores = [dot(q, kbuf[n], 1, 1) * SCALE_LOG2 for q, n in zip(qs, named)]
        dprobs = [dot(g, vbuf[n], 1, 1) for g, n in zip(gs, named)]
        expo = [jnp.exp2(s - jnp.max(s, axis=-1, keepdims=True)) for s in scores]
        probs = [e * (1.0 / jnp.sum(e, axis=-1, keepdims=True)) for e in expo]
        probs_low = [p.astype(BF) for p in probs]
        att = [dot(p, vbuf[n], 1, 0).astype(BF) for p, n in zip(probs_low, named)]
        for r, a in zip(rows, att):
            att_ref[r, :] = a
        delta = [
            jnp.sum(g.astype(F32) * a.astype(F32), axis=-1, keepdims=True) for g, a in zip(gs, att)
        ]
        ds = [(p * (d - t)).astype(BF) for p, d, t in zip(probs, dprobs, delta)]
        for r, d, n in zip(rows, ds, named):
            gq_ref[r, :] = (dot(d, kbuf[n], 1, 0) * SCALE).astype(BF)
        value_terms = [dot(p, g, 0, 0) for p, g in zip(probs_low, gs)]
        key_terms = [dot(d, q, 0, 0) for d, q in zip(ds, qs)]
        for n, vt, kt in zip(named, value_terms, key_terms):
            dv[n] += vt
            dk[n] += kt

        @pl.when(inner == steps_per_part - 1)
        def _():
            token_store(part).start()

        return 0

    lax.fori_loop(0, X * steps_per_part, body, 0)

    stores = []
    middle = HALF // 2
    pieces = (
        (HALF + N_EARLY, SLOTS, 0, 0),
        (HALF, HALF + N_EARLY, 1, 0),
        (0, middle, 2, 0),
        (middle, HALF, 2, middle),
    )
    for piece, (first, last, out, at) in enumerate(pieces):
        for which, (sums, outs) in enumerate(((dk, dk_outs), (dv, dv_outs))):

            def finish(i, _):
                value = sums[i]
                low[which, i] = (value * SCALE if which == 0 else value).astype(BF)
                return 0

            lax.fori_loop(first, last, finish, 0, unroll=4)
            count = last - first
            store = pltpu.make_async_copy(
                low.at[which, pl.ds(first, count)],
                outs[out].at[pl.ds(at, count)],
                s_sems.at[2 * piece + which],
            )
            store.start()
            stores.append(store)
    for store in stores:
        store.wait()
    for part in range(X):
        token_store(part).wait()


def attention(ids, tokens, parts):
    hbm = pl.BlockSpec(memory_space=pl.ANY)
    sums = [
        jax.ShapeDtypeStruct((n, NBLEN, HS), BF) for n in (N_LATE, N_EARLY, HALF)
    ]
    low = pltpu.VMEM((SLOTS, NBLEN, HS), BF)
    wide = pltpu.VMEM((SLOTS, NBLEN, HS), F32)
    dma = pltpu.SemaphoreType.DMA
    return pl.pallas_call(
        attention_kernel,
        grid_spec=pltpu.PrefetchScalarGridSpec(
            num_scalar_prefetch=1,
            grid=(1,),
            in_specs=[hbm] * 9,
            out_specs=[hbm] * 7,
            scratch_shapes=[
                pltpu.VMEM(tokens.shape, BF),
                low,
                low,
                pltpu.VMEM(tokens.shape, BF),
                wide,
                wide,
                pltpu.VMEM((2, SLOTS, NBLEN, HS), BF),
                dma((X,)),
                dma((8,)),
                dma((X,)),
                dma((8,)),
            ],
        ),
        out_shape=[jax.ShapeDtypeStruct(tokens.shape, BF)] + sums + sums,
        compiler_params=pltpu.CompilerParams(vmem_limit_bytes=56 * MIB),
        name="attention",
    )(ids, tokens, *parts)


def split_heads(a, b):
    tokens = a.shape[0]
    rows = 512

    def kernel(a_ref, b_ref, out):
        for h in range(X):
            at = pl.ds(h * HS, HS)
            out[h, 0] = a_ref[:, at]
            out[h, 1] = b_ref[:, at]

    wide = pl.BlockSpec((rows, X * HS), lambda i: (i, 0))
    return pl.pallas_call(
        kernel,
        grid=(tokens // rows,),
        in_specs=[wide, wide],
        out_specs=pl.BlockSpec((X, 2, rows, HS), lambda i: (0, 0, i, 0)),
        out_shape=jax.ShapeDtypeStruct((X, 2, tokens, HS), BF),
        name="split_heads",
    )(a, b)


def join_heads(a):
    tokens = a.shape[2]
    rows = 512

    def kernel(a_ref, out0, out1):
        for h in range(X):
            at = pl.ds(h * HS, HS)
            out0[:, at] = a_ref[h, 0]
            out1[:, at] = a_ref[h, 1]

    wide = pl.BlockSpec((rows, X * HS), lambda i: (i, 0))
    return pl.pallas_call(
        kernel,
        grid=(tokens // rows,),
        in_specs=[pl.BlockSpec((X, 2, rows, HS), lambda i: (0, 0, i, 0))],
        out_specs=[wide, wide],
        out_shape=[jax.ShapeDtypeStruct((tokens, X * HS), BF)] * 2,
        name="join_heads",
    )(a)


def pack_encodings(keys, values):
    def kernel(k_ref, v_ref, out):
        for h in range(HEADS):
            at = pl.ds(h * HS, HS)
            out[h, 0] = k_ref[:, :, at]
            out[h, 1] = v_ref[:, :, at]

    return pl.pallas_call(
        kernel,
        out_shape=jax.ShapeDtypeStruct((HEADS, 2, NB, PIECE, HS), BF),
        name="pack_encodings",
    )(keys, values)


def unpack_encodings(a):
    def kernel(a_ref, k_ref, v_ref):
        for h in range(HEADS):
            at = pl.ds(h * HS, HS)
            k_ref[:, :, at] = a_ref[h, 0]
            v_ref[:, :, at] = a_ref[h, 1]

    return pl.pallas_call(
        kernel,
        out_shape=[jax.ShapeDtypeStruct((NB, PIECE, HEADS * HS), BF)] * 2,
        name="unpack_encodings",
    )(a)


def final_sums(key_terms, value_terms):
    def kernel(*refs):
        out = refs[-1]
        for which in range(2):
            terms = refs[4 * which : 4 * which + 4]
            for x in range(X):
                for n in range(NB):
                    total = sum(t[x * NB + n].astype(F32) for t in terms).astype(BF)
                    for y in range(Y):
                        out[y, x, which, n] = total[y * PIECE : (y + 1) * PIECE]

    block = pl.BlockSpec((GROUP, NBLEN, HS), lambda i: (0, 0, 0))
    shape = (Y, X, 2, NB, PIECE, HS)
    return pl.pallas_call(
        kernel,
        grid=(1,),
        in_specs=[block] * 8,
        out_specs=pl.BlockSpec(shape, lambda i: (0,) * 6),
        out_shape=jax.ShapeDtypeStruct(shape, BF),
        name="final_sums",
    )(*key_terms, *value_terms)


def per_device(query, keys, values, grad_out, neighbour):
    z_self, c_self = lax.axis_index("z"), lax.axis_index("core")

    both = pack_encodings(keys, values)
    both = lax.all_to_all(both, ("head", "x"), split_axis=0, concat_axis=0, tiled=True)
    both = both.reshape(Y, X, 2, NB, PIECE, HS)
    both = jnp.transpose(both, (2, 1, 3, 0, 4, 5)).reshape(2, GROUP, NBLEN, HS)

    tokens = split_heads(query, grad_out)
    tokens = lax.all_to_all(tokens, "x", split_axis=0, concat_axis=0, tiled=True)

    parts = []
    for block in (both[0], both[1]):
        early, late = ring_gather(block)
        parts += [early, late, shift(early, "core", C, 1), shift(late, "core", C, 1)]

    table = neighbour.reshape(X, Z, C, -1)
    table = lax.dynamic_index_in_dim(table, z_self, 1, keepdims=False)
    table = lax.dynamic_index_in_dim(table, c_self, 1, keepdims=False).reshape(-1)
    owner, local = table // NB, table % NB
    owner_x, owner_z, owner_c = owner // (Z * C), (owner // C) % Z, owner % C
    other = (owner_c != c_self).astype(jnp.int32)
    offset = (owner_z - z_self) % Z
    place = sum(jnp.where(offset == o, i, 0) for i, o in enumerate(ORDER))
    ids = ((other * Z + place) * X + owner_x) * NB + local

    reply, *sums = attention(ids, tokens, parts)
    reply = lax.all_to_all(reply, "x", split_axis=0, concat_axis=0, tiled=True)

    terms = []
    for late, early, own in (sums[:3], sums[3:]):
        got_late, got_early = shift(late, "core", C, 1), shift(early, "core", C, 1)

        def block(k):
            place = ORDER.index(k)
            at = place * GROUP
            got = got_early[at : at + GROUP] if place < len(EARLY) else got_late[at - N_EARLY : at - N_EARLY + GROUP]
            return own[at : at + GROUP] + got

        right, left = ring_reduce([None] + [block(k) for k in range(1, Z)])
        terms.append((own, got_early, right, left))

    grads = final_sums(*terms).reshape(HEADS, 2, NB, PIECE, HS)
    grads, reply = lax.optimization_barrier((grads, reply))
    grads = lax.all_to_all(grads, ("head", "x"), split_axis=0, concat_axis=0, tiled=True)
    attended, grad_query = join_heads(reply)
    grad_keys, grad_values = unpack_encodings(grads)
    return attended, grad_query, grad_keys, grad_values


def solution(mesh):
    fine = Mesh(mesh.devices.reshape(X, Z, C, Y), ("x", "z", "core", "head"))
    span = ("x", "z", "core")
    tokens, encodings = P(span, "head"), P(span, "head", None)
    return jax.shard_map(
        per_device,
        mesh=fine,
        in_specs=(tokens, encodings, encodings, tokens, P()),
        out_specs=(tokens, tokens, encodings, encodings),
        check_vma=False,
    )
```
